256 devices in a mesh: row: 16 (over x_lo, y, core), col: 16 (over x_hi, z).
Axes of the slice: x: 4 (x_hi: 2, x_lo: 2; x = x_hi * 2 + x_lo), y: 4, z: 8, core: 2. Of those that a mesh axis runs over, the one named last changes fastest.
Arguments:
- top_inverse: bfloat16 [16, 16, 16, 16, 128, 128], P('row', None, None, 'col'), as said below
- upper_panel: bfloat16 [3, 16, 16, 128, 128], P(None, 'row', 'col'), may hold values from -0.25 to 0.25
- upper_pattern: int32 [3, 16, 16], P(None, 'row', 'col'), may hold values from 0 to 1
- upper_diagonal: float32 [3, 128, 128], replicated, may hold values from -6 to 6
- lower_panel: bfloat16 [8, 16, 16, 128, 128], P(None, 'row', 'col'), may hold values from -0.25 to 0.25
- lower_pattern: int32 [8, 16, 16], P(None, 'row', 'col'), may hold values from 0 to 1, as said below
- parents: int32 [8], replicated, may hold values from 0 to 2, as said below
- parent_panel: bfloat16 [8, 128, 128], replicated, may hold values from -0.5 to 0.5
- lower_diagonal: float32 [8, 128, 128], replicated, may hold values from -6 to 6
Outputs:
- upper_columns: bfloat16 [3, 16, 16, 128, 128], P(None, 'row', 'col')
- upper_blocks: float32 [3, 128, 128], replicated
- lower_columns: bfloat16 [8, 16, 16, 128, 128], P(None, 'row', 'col')
- lower_cross: float32 [8, 128, 128], replicated
- lower_blocks: float32 [8, 128, 128], replicated
The draws below stay inside these ranges and needn't reach their ends.
Inputs may be any that keep to these rules, and one draw needn't show every extreme that they name: top_inverse is symmetric: block (I, J) is the transpose of block (J, I). `lower_pattern`: A second-level pattern is zero wherever the pattern of its parent is zero. `parents`: every first-level supernode is the parent of some second-level supernode.
All inputs are finite; a program needn't handle non-finite values.
Results may differ from the reference program's by a relative error of at most 0.0041.
Values may be sent and summed in bfloat16 or wider, within the bound.
A program may use at most 128 MiB of HBM per device.

```python
import math
import jax
import jax.numpy as jnp
from jax import lax

BLOCK = 128
UPPER = 3
LOWER = 8
TOP_ROWS = 16
TOP_COLS = 16


def pattern_tables(key):
    order = jax.random.permutation(jax.random.fold_in(key, 11), LOWER)
    chosen = jax.random.randint(jax.random.fold_in(key, 14), (LOWER,), 0, UPPER).astype(jnp.int32)
    parents = chosen.at[order[:UPPER]].set(jnp.arange(UPPER, dtype=jnp.int32)).astype(jnp.int32)
    upper = jax.random.randint(jax.random.fold_in(key, 12), (UPPER, TOP_ROWS, TOP_COLS), 0, 2).astype(jnp.int32)
    keeping = jax.random.randint(jax.random.fold_in(key, 13), (LOWER, TOP_ROWS, TOP_COLS), 0, 4)
    lower = upper[parents] * (keeping > 0).astype(jnp.int32)
    return (parents, upper, lower)


def draw_parents(key, part):
    return pattern_tables(key)[0]


def draw_upper_pattern(key, part):
    return pattern_tables(key)[1]


def draw_lower_pattern(key, part):
    return pattern_tables(key)[2]


def draw_top_inverse(key, part):
    normal = jax.random.normal(key, (TOP_ROWS, TOP_COLS, TOP_ROWS, TOP_COLS, BLOCK, BLOCK), jnp.float32)
    symmetric = 0.5 * (normal + jnp.transpose(normal, (2, 3, 0, 1, 5, 4)))
    factor = 4.0 / math.sqrt(TOP_ROWS * TOP_COLS)
    return (symmetric * factor).astype(jnp.bfloat16)


def level_of(rng, shape, split, low, largest):
    gain, own = 1.0, jax.random.fold_in(rng, 6)
    for dim, shards_of in split:
        heights = jnp.exp(jax.random.uniform(jax.random.fold_in(own, dim), (shards_of,), jnp.float32, low / len(split), largest / len(split)))
        gain = gain * jnp.repeat(heights, shape[dim] // shards_of).reshape([-1 if axis == dim else 1 for axis in range(len(shape))])
    return gain


def noise(rng, dims, scale, reach, split=(), kind=jnp.bfloat16):
    array = scale * jax.random.normal(rng, dims, jnp.float32)
    if split:
        array = array * level_of(rng, dims, split, -0.22, 0.18)
    return jnp.clip(array, -reach, reach).astype(kind)


def setup_inputs(seed: int = 0) -> dict:
    splits = jax.random.split(jax.random.key(seed), 10)
    return {
        "top_inverse": draw_top_inverse(jax.random.fold_in(splits[9], 71), 0),
        "upper_panel": noise(splits[1], (UPPER, TOP_ROWS, TOP_COLS, BLOCK, BLOCK), (BLOCK * 4) ** -0.5, 0.25, ((1, 16), (2, 16))),
        "upper_pattern": draw_upper_pattern(jax.random.fold_in(splits[9], 71), 0),
        "upper_diagonal": noise(splits[3], (UPPER, BLOCK, BLOCK), 1.0, 6.0, (), jnp.float32),
        "lower_panel": noise(splits[4], (LOWER, TOP_ROWS, TOP_COLS, BLOCK, BLOCK), (BLOCK * 4) ** -0.5, 0.25, ((1, 16), (2, 16))),
        "lower_pattern": draw_lower_pattern(jax.random.fold_in(splits[9], 71), 0),
        "parents": draw_parents(jax.random.fold_in(splits[9], 71), 0),
        "parent_panel": noise(splits[7], (LOWER, BLOCK, BLOCK), BLOCK ** -0.5, 0.5),
        "lower_diagonal": noise(splits[8], (LOWER, BLOCK, BLOCK), 1.0, 6.0, (), jnp.float32),
    }


HIGH = lax.Precision.HIGHEST


def column_product(top_inverse, masked):
    wide = masked.astype(jnp.float32)

    def one_slab(top_slab):
        return jnp.einsum("ibjxy,kbjyz->kixz", top_slab.astype(jnp.float32), wide, precision=HIGH)

    stacked = lax.map(one_slab, top_inverse)
    return jnp.transpose(stacked, (1, 0, 2, 3, 4))


def reference(top_inverse, upper_panel, upper_pattern, upper_diagonal, lower_panel, lower_pattern, parents, parent_panel, lower_diagonal):
    upper_mask = upper_pattern.astype(jnp.float32)[:, :, :, None, None]
    upper_masked = upper_panel * upper_mask.astype(jnp.bfloat16)
    upper_product = column_product(top_inverse, upper_masked)
    upper_columns = (-upper_product * upper_mask).astype(jnp.bfloat16)
    upper_blocks = upper_diagonal - jnp.einsum("ktsxy,ktsxz->kyz", upper_masked.astype(jnp.float32), upper_columns.astype(jnp.float32), precision=HIGH)
    lower_mask = lower_pattern.astype(jnp.float32)[:, :, :, None, None]
    lower_masked = lower_panel * lower_mask.astype(jnp.bfloat16)
    lower_product = column_product(top_inverse, lower_masked)
    selected = jnp.take(upper_columns, parents.astype(jnp.int32), axis=0).astype(jnp.float32)
    panel_wide = parent_panel.astype(jnp.float32)
    extension = jnp.einsum("mtsxy,myz->mtsxz", selected, panel_wide, precision=HIGH)
    lower_columns = (-(lower_product + extension) * lower_mask).astype(jnp.bfloat16)
    parent_blocks = jnp.take(upper_blocks, parents.astype(jnp.int32), axis=0)
    lower_cross = -jnp.einsum("mtsxy,mtsxz->myz", selected, lower_masked.astype(jnp.float32), precision=HIGH) - jnp.einsum("mxy,myz->mxz", parent_blocks, panel_wide, precision=HIGH)
    lower_blocks = lower_diagonal - jnp.einsum("mtsxy,mtsxz->myz", lower_masked.astype(jnp.float32), lower_columns.astype(jnp.float32), precision=HIGH) - jnp.einsum("myx,myz->mxz", panel_wide, lower_cross, precision=HIGH)
    return (upper_columns, upper_blocks, lower_columns, lower_cross, lower_blocks)
```

```python
import functools

import jax
import jax.numpy as jnp
from jax import lax
from jax.experimental import pallas as pl
from jax.experimental.pallas import tpu as pltpu
from jax.sharding import PartitionSpec as P

HIGH = lax.Precision.HIGHEST
MESH = pl.DeviceIdType.MESH
F32 = jnp.float32
BF16 = jnp.bfloat16

XL, Y, XH, Z = 2, 4, 2, 8
COLS = XH * Z
PLANE = XH * XL * Y
BLOCK = 128
UPPER, LOWER = 3, 8
PANELS = UPPER + LOWER
UP, DOWN = Z // 2, Z // 2 - 1

CHUNKS = ((0, 1), (1, 2), (3, 2), (5, 2), (7, 2), (9, 2))
STARTS = (0, 1, 3, 5, 7, 9)
SPREAD = (False, False, False, False, False, False)
NC = len(CHUNKS)
FIRST_ROWS = 1536
SECOND_ROWS = LOWER * BLOCK


def kernel(
    top_hbm,
    upper_hbm,
    upper_pattern,
    upper_diagonal_hbm,
    lower_hbm,
    lower_pattern,
    parents,
    parent_panel_hbm,
    lower_diagonal_hbm,
    upper_columns,
    upper_blocks,
    lower_columns,
    lower_cross,
    lower_blocks,
    top,
    panel,
    parent_panel,
    upper_diagonal,
    lower_diagonal,
    masked,
    gathered,
    core_out,
    core_in,
    own_sum,
    y_out,
    y_in,
    x_sum,
    x_in,
    columns_t,
    extension_t,
    base,
    first,
    second,
    load_sem,
    ring_send,
    ring_recv,
    spread_send,
    spread_recv,
    core_send,
    core_recv,
    y_send,
    y_recv,
    x_send,
    x_recv,
    first_sems,
    second_sems,
):
    row = lax.axis_index("row")
    col = lax.axis_index("col")
    co = row % 2
    y = (row // 2) % Y
    xl = row // (2 * Y)
    z = col % Z
    xh = col // Z

    def device(dxl=0, dy=0, dco=0, dxh=0, dz=0):
        r = (((xl + dxl) % XL) * Y + (y + dy) % Y) * 2 + (co + dco) % 2
        c = ((xh + dxh) % XH) * Z + (z + dz) % Z
        return (r, c)

    plane_offsets = [
        (dxh, dxl, dy)
        for dxh in range(XH)
        for dxl in range(XL)
        for dy in range(Y)
        if (dxh, dxl, dy) != (0, 0, 0)
    ]

    loads = []

    def load(src, dst):
        copy = pltpu.make_async_copy(src, dst, load_sem.at[len(loads)])
        copy.start()
        loads.append(copy)

    load(upper_hbm, panel.at[pl.ds(0, UPPER)])
    load(lower_hbm, panel.at[pl.ds(UPPER, LOWER)])
    load(top_hbm.at[:, :, 1 - co], top.at[1])
    load(top_hbm.at[:, :, co], top.at[0])
    load(parent_panel_hbm, parent_panel)
    load(upper_diagonal_hbm, upper_diagonal)
    load(lower_diagonal_hbm, lower_diagonal)

    barrier = pltpu.get_barrier_semaphore()
    partners = [device(dxh=a, dxl=b, dy=c) for a, b, c in plane_offsets]
    partners += [device(dz=d) for d in range(1, Z)] + [device(dco=1)]
    for partner in partners:
        pl.semaphore_signal(barrier, 1, device_id=partner, device_id_type=MESH)

    loads[0].wait()
    loads[1].wait()
    for k in range(PANELS):
        if k < UPPER:
            mask = upper_pattern[k, 0, 0].astype(F32)
        else:
            mask = lower_pattern[k - UPPER, 0, 0].astype(F32)
        wide = panel[k].astype(F32) * mask
        masked[k] = wide.astype(BF16)
        gathered[col, k] = wide.T.astype(BF16)

    pl.semaphore_wait(barrier, len(partners))

    started = []

    def send(src, dst, send_sem, recv_sem, to):
        copy = pltpu.make_async_remote_copy(
            src_ref=src, dst_ref=dst, send_sem=send_sem, recv_sem=recv_sem,
            device_id=to, device_id_type=MESH,
        )
        copy.start()
        started.append(copy)

    def arrive(dst, send_sem, recv_sem):
        pltpu.make_async_remote_copy(
            src_ref=dst, dst_ref=dst, send_sem=send_sem, recv_sem=recv_sem,
            device_id=device(dco=1), device_id_type=MESH,
        ).wait_recv()

    def block(j, plane, dz):
        k0, nk = CHUNKS[j]
        index = ((xh + plane) % XH) * Z + (z + dz) % Z
        return gathered.at[index, pl.ds(k0, nk)]

    def spread_slot(j, dz):
        return spread_send.at[j, dz % Z], spread_recv.at[j, dz % Z]

    def spread(j, dz):
        mine = block(j, 0, dz)
        send(mine, mine, *spread_slot(j, dz), device(dxh=1))

    def ring(j, plane, way, step):
        sign = 1 - 2 * way
        if step:
            arrive(
                block(j, plane, -sign * step),
                ring_send.at[j, plane, way, step - 1],
                ring_recv.at[j, plane, way, step - 1],
            )
            if SPREAD[j]:
                spread(j, -sign * step)
        hops = UP if (way == 0) == (plane == 0) else DOWN
        if step < hops:
            mine = block(j, plane, -sign * step)
            send(
                mine,
                mine,
                ring_send.at[j, plane, way, step],
                ring_recv.at[j, plane, way, step],
                device(dz=sign),
            )

    def ring_event(j, plane, step):
        for way in (0, 1):
            hops = UP if (way == 0) == (plane == 0) else DOWN
            if step <= hops:
                ring(j, plane, way, step)

    def seed(j):
        ring_event(j, 0, 0)
        spread(j, 0)

    def seed_other(j):
        arrive(block(j, 1, 0), *spread_slot(j, 0))
        ring_event(j, 1, 0)

    def collect_spread(j):
        for dz in range(Z):
            arrive(block(j, 1, dz), *spread_slot(j, dz))

    def multiply(j):
        k0, nk = CHUNKS[j]
        ks = pl.ds(k0, nk)

        def product(half, pair):
            left = jnp.concatenate(
                [gathered[i, ks].reshape(nk * BLOCK, BLOCK) for i in range(COLS)], axis=1
            )
            right = jnp.concatenate(
                [top[half, :, 2 * pair + d].reshape(COLS * BLOCK, BLOCK) for d in range(2)],
                axis=1,
            )
            return jnp.dot(left, right, preferred_element_type=F32)

        def theirs(pair, carry):
            out = product(1, pair)
            for d in range(2):
                core_out[2 * pair + d, ks] = (
                    out[:, d * BLOCK : (d + 1) * BLOCK].reshape(nk, BLOCK, BLOCK).astype(BF16)
                )
            return carry

        def ours(pair, carry):
            out = product(0, pair)
            for d in range(2):
                own_sum[2 * pair + d, ks] = out[:, d * BLOCK : (d + 1) * BLOCK].reshape(
                    nk, BLOCK, BLOCK
                )
            return carry

        lax.fori_loop(0, XL * Y // 2, theirs, 0)
        send(
            core_out.at[:, ks], core_in.at[:, ks], core_send.at[j], core_recv.at[j],
            device(dco=1),
        )
        lax.fori_loop(0, XL * Y // 2, ours, 0)

    def add_core(j):
        k0, nk = CHUNKS[j]
        ks = pl.ds(k0, nk)
        arrive(core_in.at[:, ks], core_send.at[j], core_recv.at[j])

        def body(q, carry):
            total = own_sum[q, ks] + core_in[q, ks].astype(F32)
            own_sum[q, ks] = total
            y_out[q // Y, q % Y, ks] = total.astype(BF16)
            return carry

        lax.fori_loop(0, XL * Y, body, 0)
        for dy in (2, 1, 3):
            send(
                y_out.at[:, (y + dy) % Y, ks],
                y_in.at[dy - 1, :, ks],
                y_send.at[j, dy - 1],
                y_recv.at[j, dy - 1],
                device(dy=dy),
            )

    def add_y(j):
        k0, nk = CHUNKS[j]
        ks = pl.ds(k0, nk)
        for dy in range(1, Y):
            arrive(y_in.at[dy - 1, :, ks], y_send.at[j, dy - 1], y_recv.at[j, dy - 1])
        for side in range(XL):
            total = own_sum[side * Y + y, ks]
            for dy in range(1, Y):
                total += y_in[dy - 1, side, ks].astype(F32)
            x_sum[side, ks] = total
        send(
            x_sum.at[1 - xl, ks], x_in.at[ks], x_send.at[j], x_recv.at[j], device(dxl=1)
        )

    def finish(j):
        k0, nk = CHUNKS[j]
        ks = pl.ds(k0, nk)
        arrive(x_in.at[ks], x_send.at[j], x_recv.at[j])
        for k in range(k0, k0 + nk):
            product_t = x_sum[xl, k] + x_in[k]
            if k < UPPER:
                mask = upper_pattern[k, 0, 0].astype(F32)
                wide = -product_t * mask
                columns_t[k] = wide.astype(BF16)
                natural = wide.T.astype(BF16)
                upper_columns[k] = natural
                first[pl.ds(k * BLOCK, BLOCK)] = jnp.dot(
                    gathered[col, k], natural, preferred_element_type=F32
                )
            else:
                m = k - UPPER
                mask = lower_pattern[m, 0, 0].astype(F32)
                natural = (-(product_t + extension_t[m]) * mask).T.astype(BF16)
                lower_columns[m] = natural
                second[pl.ds(m * BLOCK, BLOCK)] = jnp.dot(
                    gathered[col, k], natural, preferred_element_type=F32
                )

    def cross():
        loads[4].wait()
        first[pl.ds(PANELS * BLOCK, FIRST_ROWS - PANELS * BLOCK)] = jnp.zeros(
            (FIRST_ROWS - PANELS * BLOCK, BLOCK), F32
        )
        for m in range(LOWER):
            selected_t = columns_t[parents[m]]
            first[pl.ds((UPPER + m) * BLOCK, BLOCK)] = jnp.dot(
                selected_t, masked[UPPER + m], preferred_element_type=F32
            )
            panel_t = parent_panel[m].astype(F32).T.astype(BF16)
            extension_t[m] = jnp.dot(panel_t, selected_t, preferred_element_type=F32)

    class AllReduce:
        def __init__(self, array, rows, refs):
            self.array, self.rows = array, rows
            self.half, self.piece = rows // 2, rows // 2 // PLANE
            self.core_in, self.half_sum, self.plane_in, self.z_in, self.total = refs[:5]
            self.send, self.recv = refs[5:]
            self.mine = (xh * XL + xl) * Y + y

        def sems(self, i):
            return self.send.at[i], self.recv.at[i]

        def rows_of(self, half, index, count):
            return pl.ds(pl.multiple_of(half * self.half + index * self.piece, 8), count)

        def core(self):
            send(
                self.array.at[self.rows_of(1 - co, 0, self.half)],
                self.core_in,
                *self.sems(0),
                device(dco=1),
            )

        def scatter(self):
            arrive(self.core_in, *self.sems(0))
            self.half_sum[...] = (
                self.array[self.rows_of(co, 0, self.half)] + self.core_in[...]
            )
            for n, (a, b, c) in enumerate(plane_offsets):
                to = (((xh + a) % XH) * XL + (xl + b) % XL) * Y + (y + c) % Y
                send(
                    self.half_sum.at[self.rows_of(0, to, self.piece)],
                    self.plane_in.at[n],
                    *self.sems(1 + n),
                    device(dxh=a, dxl=b, dy=c),
                )

        def exchange(self):
            total = self.half_sum[self.rows_of(0, self.mine, self.piece)]
            for n in range(PLANE - 1):
                arrive(self.plane_in.at[n], *self.sems(1 + n))
                total += self.plane_in[n]
            self.z_in[z] = total
            for dz in range(1, Z):
                send(
                    self.z_in.at[z],
                    self.z_in.at[z],
                    *self.sems(PLANE + dz - 1),
                    device(dz=dz),
                )

        def gather(self):
            for dz in range(1, Z):
                arrive(self.z_in.at[(z - dz) % Z], *self.sems(PLANE + dz - 1))
            total = self.z_in[0]
            for other in range(1, Z):
                total += self.z_in[other]
            place = self.rows_of(co, self.mine, self.piece)
            self.total[place] = total
            for n, (a, b, c) in enumerate(plane_offsets):
                send(
                    self.total.at[place],
                    self.total.at[place],
                    *self.sems(PLANE + Z - 1 + n),
                    device(dxh=a, dxl=b, dy=c),
                )

        def swap(self):
            for n, (a, b, c) in enumerate(plane_offsets):
                source = (((xh - a) % XH) * XL + (xl - b) % XL) * Y + (y - c) % Y
                arrive(
                    self.total.at[self.rows_of(co, source, self.piece)],
                    *self.sems(PLANE + Z - 1 + n),
                )
            ours = self.rows_of(co, 0, self.half)
            send(
                self.total.at[ours], self.total.at[ours], *self.sems(2 * PLANE + Z - 2),
                device(dco=1),
            )

        def end(self):
            arrive(
                self.total.at[self.rows_of(1 - co, 0, self.half)],
                *self.sems(2 * PLANE + Z - 2),
            )

    reduce_first = AllReduce(first, FIRST_ROWS, first_sems)
    reduce_second = AllReduce(second, SECOND_ROWS, second_sems)

    def first_outputs():
        reduce_first.end()
        loads[5].wait()
        loads[6].wait()
        for k in range(UPPER):
            upper_blocks[k] = upper_diagonal[k] - reduce_first.total[pl.ds(k * BLOCK, BLOCK)]
        for m in range(LOWER):
            wide = parent_panel[m].astype(F32)
            value = -reduce_first.total[pl.ds((UPPER + m) * BLOCK, BLOCK)] - jnp.dot(
                upper_blocks[parents[m]], wide, precision=HIGH, preferred_element_type=F32
            )
            lower_cross[m] = value
            base[m] = lower_diagonal[m] - jnp.dot(
                wide.T, value, precision=HIGH, preferred_element_type=F32
            )

    def last_outputs():
        reduce_second.end()
        for m in range(LOWER):
            lower_blocks[m] = base[m] - reduce_second.total[pl.ds(m * BLOCK, BLOCK)]

    events = []

    def at(time, order, what):
        events.append((time, order, len(events), what))

    def wait_top(j):
        if j == 0:
            loads[2].wait()
            loads[3].wait()
        multiply(j)

    for j, start in enumerate(STARTS):
        at(start, 0, functools.partial(seed, j))
        for step in range(1, UP + 1):
            at(start + step, 0, functools.partial(ring_event, j, 0, step))
        if SPREAD[j]:
            ready = start + UP + 1
            at(ready, 0, functools.partial(collect_spread, j))
        else:
            ready = start + 1 + UP
            at(start + 1, 1, functools.partial(seed_other, j))
            for step in range(1, UP + 1):
                at(start + 1 + step, 1, functools.partial(ring_event, j, 1, step))
        at(ready, 4, functools.partial(wait_top, j))
        at(ready + 1, 3, functools.partial(add_core, j))
        at(ready + 2, 2, functools.partial(add_y, j))
        at(ready + 3, 2, functools.partial(finish, j))
    last_upper = max(j for j in range(NC) if CHUNKS[j][0] < UPPER)
    when = STARTS[last_upper] + UP + 1 + 3
    at(when, 2.5, cross)
    at(when, 2.6, reduce_first.core)
    at(when + 1, 2.6, reduce_first.scatter)
    at(when + 2, 2.6, reduce_first.exchange)
    at(when + 3, 2.6, reduce_first.gather)
    at(when + 4, 2.6, reduce_first.swap)
    at(when + 5, 2.6, first_outputs)
    end = max(STARTS[-1] + UP + 1 + 3, when + 5)
    at(end, 5, reduce_second.core)
    at(end + 1, 2.6, reduce_second.scatter)
    at(end + 2, 2.6, reduce_second.exchange)
    at(end + 3, 2.6, reduce_second.gather)
    at(end + 4, 2.6, reduce_second.swap)
    at(end + 5, 2.6, last_outputs)
    for _, _, _, what in sorted(events, key=lambda event: event[:3]):
        what()

    for copy in started:
        copy.wait_send()


def reduce_scratch(rows):
    half = rows // 2
    piece = half // PLANE
    count = 2 * PLANE + Z - 1
    return [
        pltpu.VMEM((half, BLOCK), F32),
        pltpu.VMEM((half, BLOCK), F32),
        pltpu.VMEM((PLANE - 1, piece, BLOCK), F32),
        pltpu.VMEM((Z, piece, BLOCK), F32),
        pltpu.VMEM((rows, BLOCK), F32),
        pltpu.SemaphoreType.DMA((count,)),
        pltpu.SemaphoreType.DMA((count,)),
    ]


def per_device(
    top_inverse,
    upper_panel,
    upper_pattern,
    upper_diagonal,
    lower_panel,
    lower_pattern,
    parents,
    parent_panel,
    lower_diagonal,
):
    square = (BLOCK, BLOCK)
    anywhere = pl.BlockSpec(memory_space=pl.ANY)
    scalars = pl.BlockSpec(memory_space=pltpu.SMEM)
    vector = pl.BlockSpec(memory_space=pltpu.VMEM)
    outs = pl.pallas_call(
        kernel,
        out_shape=(
            jax.ShapeDtypeStruct((UPPER, *square), BF16),
            jax.ShapeDtypeStruct((UPPER, *square), F32),
            jax.ShapeDtypeStruct((LOWER, *square), BF16),
            jax.ShapeDtypeStruct((LOWER, *square), F32),
            jax.ShapeDtypeStruct((LOWER, *square), F32),
        ),
        in_specs=[anywhere, anywhere, scalars, anywhere, anywhere, scalars, scalars, anywhere, anywhere],
        out_specs=(vector,) * 5,
        scratch_shapes=[
            pltpu.VMEM((2, COLS, XL * Y, *square), BF16),
            pltpu.VMEM((PANELS, *square), BF16),
            pltpu.VMEM((LOWER, *square), BF16),
            pltpu.VMEM((UPPER, *square), F32),
            pltpu.VMEM((LOWER, *square), F32),
            pltpu.VMEM((PANELS, *square), BF16),
            pltpu.VMEM((COLS, PANELS, *square), BF16),
            pltpu.VMEM((XL * Y, PANELS, *square), BF16),
            pltpu.VMEM((XL * Y, PANELS, *square), BF16),
            pltpu.VMEM((XL * Y, PANELS, *square), F32),
            pltpu.VMEM((XL, Y, PANELS, *square), BF16),
            pltpu.VMEM((Y - 1, XL, PANELS, *square), BF16),
            pltpu.VMEM((XL, PANELS, *square), F32),
            pltpu.VMEM((PANELS, *square), F32),
            pltpu.VMEM((UPPER, *square), BF16),
            pltpu.VMEM((LOWER, *square), F32),
            pltpu.VMEM((LOWER, *square), F32),
            pltpu.VMEM((FIRST_ROWS, BLOCK), F32),
            pltpu.VMEM((SECOND_ROWS, BLOCK), F32),
            pltpu.SemaphoreType.DMA((7,)),
            pltpu.SemaphoreType.DMA((NC, 2, 2, UP)),
            pltpu.SemaphoreType.DMA((NC, 2, 2, UP)),
            pltpu.SemaphoreType.DMA((NC, Z)),
            pltpu.SemaphoreType.DMA((NC, Z)),
            pltpu.SemaphoreType.DMA((NC,)),
            pltpu.SemaphoreType.DMA((NC,)),
            pltpu.SemaphoreType.DMA((NC, Y - 1)),
            pltpu.SemaphoreType.DMA((NC, Y - 1)),
            pltpu.SemaphoreType.DMA((NC,)),
            pltpu.SemaphoreType.DMA((NC,)),
            reduce_scratch(FIRST_ROWS),
            reduce_scratch(SECOND_ROWS),
        ],
        compiler_params=pltpu.CompilerParams(
            collective_id=0, has_side_effects=True, vmem_limit_bytes=62 * 1024 * 1024
        ),
        name="sweep",
    )(
        top_inverse.reshape(COLS, XL * Y, 2, *square),
        upper_panel.reshape(UPPER, *square),
        upper_pattern,
        upper_diagonal,
        lower_panel.reshape(LOWER, *square),
        lower_pattern,
        parents,
        parent_panel,
        lower_diagonal,
    )
    return (
        outs[0].reshape(UPPER, 1, 1, *square),
        outs[1],
        outs[2].reshape(LOWER, 1, 1, *square),
        outs[3],
        outs[4],
    )


def solution(mesh):
    return jax.shard_map(
        per_device,
        mesh=mesh,
        in_specs=(
            P("row", None, None, "col", None, None),
            P(None, "row", "col", None, None),
            P(None, "row", "col"),
            P(),
            P(None, "row", "col", None, None),
            P(None, "row", "col"),
            P(),
            P(),
            P(),
        ),
        out_specs=(
            P(None, "row", "col", None, None),
            P(),
            P(None, "row", "col", None, None),
            P(),
            P(),
        ),
        check_vma=False,
    )
```

```python
import functools

import jax
import jax.numpy as jnp
from jax import lax
from jax.experimental import pallas as pl
from jax.experimental.pallas import tpu as pltpu
from jax.sharding import PartitionSpec as P

HIGH = lax.Precision.HIGHEST
MESH = pl.DeviceIdType.MESH
F32 = jnp.float32
BF16 = jnp.bfloat16

XL, Y, XH, Z = 2, 4, 2, 8
COLS = XH * Z
PLANE = XH * XL * Y
BLOCK = 128
UPPER, LOWER = 3, 8
PANELS = UPPER + LOWER
UP, DOWN = Z // 2, Z // 2 - 1

CHUNKS = ((0, 1), (1, 2), (3, 2), (5, 2), (7, 2), (9, 1), (10, 1))
SPREAD = (True, False, True, True, False, True, False)
NC = len(CHUNKS)
LATE = 4
ORDER = (
    ("seed", 0), ("seed", 1), ("seed", 2), ("ring", 0, 0, 1), ("ring", 1, 0, 1),
    ("seed_other", 1), ("ring", 2, 0, 1), ("ring", 0, 0, 2), ("ring", 1, 0, 2),
    ("ring", 1, 1, 1), ("ring", 2, 0, 2), ("ring", 0, 0, 3), ("ring", 1, 0, 3),
    ("ring", 1, 1, 2), ("ring", 2, 0, 3), ("ring", 0, 0, 4), ("ring", 1, 0, 4), ("seed", 3),
    ("ring", 1, 1, 3), ("ring", 2, 0, 4), ("seed", 4), ("m0", 0), ("ring", 3, 0, 1), ("m1", 0),
    ("ring", 1, 1, 4), ("m0", 1), ("ring", 3, 0, 2), ("ring", 4, 0, 1), ("seed_other", 4),
    ("e", 0), ("m1", 1), ("m0", 2), ("ring", 3, 0, 3), ("e", 1), ("m1", 2), ("ring", 4, 0, 2),
    ("ring", 4, 1, 1), ("f", 0), ("e", 2), ("ring", 3, 0, 4), ("seed", 5), ("ring", 4, 0, 3),
    ("h", 0), ("ring", 4, 1, 2), ("ring", 5, 0, 1), ("m0", 3), ("ring", 4, 0, 4), ("seed", 6),
    ("f", 1), ("ring", 4, 1, 3), ("m1", 3), ("ring", 5, 0, 2), ("ring", 6, 0, 1), ("e", 3),
    ("seed_other", 6), ("ring", 4, 1, 4), ("m0", 4), ("ring", 5, 0, 3), ("ring", 6, 0, 2),
    ("h", 1), ("ring", 6, 1, 1), ("cross",), ("f", 2), ("a", 0), ("m1", 4), ("ring", 5, 0, 4),
    ("ring", 6, 0, 3), ("e", 4), ("ring", 6, 1, 2), ("a", 1), ("ring", 6, 0, 4), ("f", 3),
    ("h", 2), ("ring", 6, 1, 3), ("m0", 5), ("ring", 6, 1, 4), ("m1", 5), ("m0", 6), ("e", 5),
    ("m1", 6), ("f", 4), ("e", 6), ("h", 3), ("b", 0), ("h", 4), ("a", 2), ("f", 5), ("f", 6),
    ("h", 5), ("h", 6), ("c", 0), ("a", 3), ("b", 1), ("b", 2), ("c", 1), ("a", 4), ("c", 2),
    ("a", 5), ("b", 3), ("c", 3),
)
FIRST_ROWS = 1536
SECOND_ROWS = (LOWER - LATE) * BLOCK
THIRD_ROWS = LATE * BLOCK
GROUP = 2 * PLANE


def kernel(
    top_hbm,
    upper_hbm,
    upper_pattern,
    upper_diagonal_hbm,
    lower_hbm,
    lower_pattern,
    parents,
    parent_panel_hbm,
    lower_diagonal_hbm,
    upper_columns_hbm,
    upper_blocks_hbm,
    lower_columns_hbm,
    lower_cross_hbm,
    lower_blocks_hbm,
    upper_columns,
    upper_blocks,
    lower_columns,
    lower_cross,
    lower_blocks,
    store_sem,
    top,
    panel,
    parent_panel,
    upper_diagonal,
    lower_diagonal,
    masked,
    gathered,
    core_out,
    core_in,
    own_sum,
    y_out,
    y_in,
    x_sum,
    x_in,
    columns_t,
    extension_t,
    base,
    first,
    second,
    third,
    load_sem,
    ring_send,
    ring_recv,
    spread_recv,
    core_send,
    core_recv,
    y_send,
    y_recv,
    x_send,
    x_recv,
    first_sems,
    second_sems,
    third_sems,
):
    row = lax.axis_index("row")
    col = lax.axis_index("col")
    co = row % 2
    y = (row // 2) % Y
    xl = row // (2 * Y)
    z = col % Z
    xh = col // Z

    def device(dxl=0, dy=0, dco=0, dxh=0, dz=0):
        r = (((xl + dxl) % XL) * Y + (y + dy) % Y) * 2 + (co + dco) % 2
        c = ((xh + dxh) % XH) * Z + (z + dz) % Z
        return (r, c)

    plane_offsets = [
        (dxh, dxl, dy)
        for dxh in range(XH)
        for dxl in range(XL)
        for dy in range(Y)
        if (dxh, dxl, dy) != (0, 0, 0)
    ]

    loads = []

    def load(src, dst):
        copy = pltpu.make_async_copy(src, dst, load_sem.at[len(loads)])
        copy.start()
        loads.append(copy)

    load(upper_hbm, panel.at[pl.ds(0, UPPER)])
    load(lower_hbm, panel.at[pl.ds(UPPER, LOWER)])
    load(top_hbm.at[:, :, 1 - co], top.at[1])
    load(top_hbm.at[:, :, co], top.at[0])
    load(parent_panel_hbm, parent_panel)
    load(upper_diagonal_hbm, upper_diagonal)
    load(lower_diagonal_hbm, lower_diagonal)

    stores = []

    def store(src, dst):
        copy = pltpu.make_async_copy(src, dst, store_sem.at[len(stores)])
        copy.start()
        stores.append(copy)

    barrier = pltpu.get_barrier_semaphore()
    partners = [device(dxh=a, dxl=b, dy=c) for a, b, c in plane_offsets]
    partners += [device(dz=d) for d in range(1, Z)] + [device(dco=1)]
    for partner in partners:
        pl.semaphore_signal(barrier, 1, device_id=partner, device_id_type=MESH)

    loads[0].wait()
    loads[1].wait()
    for k in range(PANELS):
        if k < UPPER:
            mask = upper_pattern[k].astype(F32)
        else:
            mask = lower_pattern[k - UPPER].astype(F32)
        wide = panel[k].astype(F32) * mask
        masked[k] = wide.astype(BF16)
        gathered[col, k] = wide.T.astype(BF16)

    pl.semaphore_wait(barrier, len(partners))

    sent = []

    def send(src, dst, send_sem, recv_sem, to):
        pltpu.make_async_remote_copy(
            src_ref=src, dst_ref=dst, send_sem=send_sem, recv_sem=recv_sem,
            device_id=to, device_id_type=MESH,
        ).start()

    def leave(extent, send_sem):
        sent.append((extent, send_sem))

    def arrive(extent, recv_sem):
        pltpu.make_async_remote_copy(
            src_ref=extent, dst_ref=extent, send_sem=recv_sem, recv_sem=recv_sem,
            device_id=device(dco=1), device_id_type=MESH,
        ).wait_recv()

    def block(j, plane, dz):
        k0, nk = CHUNKS[j]
        index = ((xh + plane) % XH) * Z + (z + dz) % Z
        return gathered.at[index, pl.ds(k0, nk)]

    def blocks(j, count):
        k0, nk = CHUNKS[j]
        return gathered.at[pl.ds(0, count), pl.ds(k0, nk)]

    def spread(j, dz):
        mine = block(j, 0, dz)
        send(mine, mine, ring_send.at[j], spread_recv.at[j], device(dxh=1))

    def ring_event(j, plane, step):
        hops = {1: UP, -1: DOWN} if plane == 0 else {1: DOWN, -1: UP}
        if step:
            ways = [way for way in hops if step <= hops[way]]
            arrive(blocks(j, len(ways)), ring_recv.at[j, plane, step - 1])
            if SPREAD[j]:
                for way in ways:
                    spread(j, -way * step)
        for way in hops:
            if step < hops[way]:
                mine = block(j, plane, -way * step)
                send(mine, mine, ring_send.at[j], ring_recv.at[j, plane, step], device(dz=way))

    def seed(j):
        ring_event(j, 0, 0)
        spread(j, 0)
        leave(blocks(j, COLS - 1), ring_send.at[j])

    def seed_other(j):
        arrive(blocks(j, 1), spread_recv.at[j])
        ring_event(j, 1, 0)

    def collect_spread(j):
        arrive(blocks(j, Z), spread_recv.at[j])

    def multiply(j, part):
        k0, nk = CHUNKS[j]
        ks = pl.ds(k0, nk)

        def product(half, pair):
            left = jnp.concatenate(
                [gathered[i, ks].reshape(nk * BLOCK, BLOCK) for i in range(COLS)], axis=1
            )
            right = jnp.concatenate(
                [top[half, :, 2 * pair + d].reshape(COLS * BLOCK, BLOCK) for d in range(2)],
                axis=1,
            )
            return jnp.dot(left, right, preferred_element_type=F32)

        def theirs(pair, carry):
            out = product(1, pair)
            for d in range(2):
                core_out[2 * pair + d, ks] = (
                    out[:, d * BLOCK : (d + 1) * BLOCK].reshape(nk, BLOCK, BLOCK).astype(BF16)
                )
            return carry

        def ours(pair, carry):
            out = product(0, pair)
            for d in range(2):
                own_sum[2 * pair + d, ks] = out[:, d * BLOCK : (d + 1) * BLOCK].reshape(
                    nk, BLOCK, BLOCK
                )
            return carry

        if part == 0:
            lax.fori_loop(0, XL * Y // 2, theirs, 0)
            send(
                core_out.at[:, ks], core_in.at[:, ks], core_send.at[0], core_recv.at[j],
                device(dco=1),
            )
        else:
            lax.fori_loop(0, XL * Y // 2, ours, 0)

    def add_core(j):
        k0, nk = CHUNKS[j]
        ks = pl.ds(k0, nk)
        arrive(core_in.at[:, ks], core_recv.at[j])

        def body(q, carry):
            total = own_sum[q, ks] + core_in[q, ks].astype(F32)
            own_sum[q, ks] = total
            y_out[q // Y, q % Y, ks] = total.astype(BF16)
            return carry

        lax.fori_loop(0, XL * Y, body, 0)
        for dy in (2, 1, 3):
            send(
                y_out.at[:, (y + dy) % Y, ks],
                y_in.at[dy - 1, :, ks],
                y_send.at[0],
                y_recv.at[j],
                device(dy=dy),
            )

    def add_y(j):
        k0, nk = CHUNKS[j]
        ks = pl.ds(k0, nk)
        arrive(y_in.at[:, :, ks], y_recv.at[j])
        for side in range(XL):
            total = own_sum[side * Y + y, ks]
            for dy in range(1, Y):
                total += y_in[dy - 1, side, ks].astype(F32)
            x_sum[side, ks] = total
        send(
            x_sum.at[1 - xl, ks], x_in.at[ks], x_send.at[0], x_recv.at[j], device(dxl=1)
        )

    def finish(j):
        k0, nk = CHUNKS[j]
        ks = pl.ds(k0, nk)
        arrive(x_in.at[ks], x_recv.at[j])
        for k in range(k0, k0 + nk):
            product_t = x_sum[xl, k] + x_in[k]
            if k < UPPER:
                mask = upper_pattern[k].astype(F32)
                wide = -product_t * mask
                columns_t[k] = wide.astype(BF16)
                natural = wide.T.astype(BF16)
                upper_columns[k] = natural
                first[pl.ds(k * BLOCK, BLOCK)] = jnp.dot(
                    gathered[col, k], natural, preferred_element_type=F32
                )
            else:
                m = k - UPPER
                mask = lower_pattern[m].astype(F32)
                natural = (-(product_t + extension_t[m]) * mask).T.astype(BF16)
                lower_columns[m] = natural
                sums, at_row = (second, m) if m < LOWER - LATE else (third, m - LOWER + LATE)
                sums[pl.ds(at_row * BLOCK, BLOCK)] = jnp.dot(
                    gathered[col, k], natural, preferred_element_type=F32
                )
        if k0 < UPPER:
            store(upper_columns.at[ks], upper_columns_hbm.at[ks])
        else:
            ms = pl.ds(k0 - UPPER, nk)
            store(lower_columns.at[ms], lower_columns_hbm.at[ms])

    def cross():
        loads[4].wait()
        first[pl.ds(PANELS * BLOCK, FIRST_ROWS - PANELS * BLOCK)] = jnp.zeros(
            (FIRST_ROWS - PANELS * BLOCK, BLOCK), F32
        )
        for m in range(LOWER):
            selected_t = columns_t[parents[m]]
            first[pl.ds((UPPER + m) * BLOCK, BLOCK)] = jnp.dot(
                selected_t, masked[UPPER + m], preferred_element_type=F32
            )
            panel_t = parent_panel[m].astype(F32).T.astype(BF16)
            extension_t[m] = jnp.dot(panel_t, selected_t, preferred_element_type=F32)

    class AllReduce:
        def __init__(self, array, rows, refs):
            self.array, self.rows = array, rows
            self.half, self.piece = rows // 2, rows // 2 // PLANE
            self.core_in, self.half_sum, self.plane_in, self.z_in, self.total = refs[:5]
            self.send, self.recv = refs[5:]
            self.mine = (xh * XL + xl) * Y + y

        def sems(self, i):
            return self.send.at[i], self.recv.at[i]

        def rows_of(self, half, index, count):
            return pl.ds(pl.multiple_of(half * self.half + index * self.piece, 8), count)

        def core(self):
            send(
                self.array.at[self.rows_of(1 - co, 0, self.half)],
                self.core_in,
                *self.sems(0),
                device(dco=1),
            )
            leave(self.core_in, self.send.at[0])

        def scatter(self):
            arrive(self.core_in, self.recv.at[0])
            self.half_sum[...] = (
                self.array[self.rows_of(co, 0, self.half)] + self.core_in[...]
            )
            for n, (a, b, c) in enumerate(plane_offsets):
                to = (((xh + a) % XH) * XL + (xl + b) % XL) * Y + (y + c) % Y
                send(
                    self.half_sum.at[self.rows_of(0, to, self.piece)],
                    self.plane_in.at[n],
                    *self.sems(1),
                    device(dxh=a, dxl=b, dy=c),
                )
            leave(self.plane_in, self.send.at[1])

        def exchange(self):
            arrive(self.plane_in, self.recv.at[1])
            total = self.half_sum[self.rows_of(0, self.mine, self.piece)]
            for n in range(PLANE - 1):
                total += self.plane_in[n]
            self.z_in[z] = total
            for dz in (4, 3, 5, 2, 6, 1, 7):
                send(self.z_in.at[z], self.z_in.at[z], *self.sems(2), device(dz=dz))
            leave(self.z_in.at[pl.ds(0, Z - 1)], self.send.at[2])

        def gather(self):
            arrive(self.z_in.at[pl.ds(0, Z - 1)], self.recv.at[2])
            total = self.z_in[0]
            for other in range(1, Z):
                total += self.z_in[other]
            place = self.rows_of(co, self.mine, self.piece)
            self.total[place] = total
            for a, b, c in plane_offsets:
                send(
                    self.total.at[place],
                    self.total.at[place],
                    *self.sems(3),
                    device(dxh=a, dxl=b, dy=c),
                )
            leave(self.plane_in, self.send.at[3])

        def swap(self):
            arrive(self.plane_in, self.recv.at[3])
            ours = self.rows_of(co, 0, self.half)
            send(self.total.at[ours], self.total.at[ours], *self.sems(4), device(dco=1))
            leave(self.core_in, self.send.at[4])

        def end(self):
            arrive(self.core_in, self.recv.at[4])

    group_offsets = [(0, 0, 0, 1)] + [
        (*offset, d) for offset in plane_offsets for d in range(2)
    ]

    class ShortAllReduce:
        def __init__(self, array, rows, refs):
            self.array, self.piece = array, rows // GROUP
            self.group_in, self.z_in, self.total, self.send, self.recv = refs

        def sems(self, i):
            return self.send.at[i], self.recv.at[i]

        def place(self, a, b, c, d):
            index = ((((xh + a) % XH) * XL + (xl + b) % XL) * Y + (y + c) % Y) * 2
            index = index + (co + d) % 2
            return pl.ds(pl.multiple_of(index * self.piece, 8), self.piece)

        def scatter(self):
            for n, (a, b, c, d) in enumerate(group_offsets):
                send(
                    self.array.at[self.place(a, b, c, d)],
                    self.group_in.at[n],
                    *self.sems(0),
                    device(dxh=a, dxl=b, dy=c, dco=d),
                )
            leave(self.group_in, self.send.at[0])

        def exchange(self):
            arrive(self.group_in, self.recv.at[0])
            total = self.array[self.place(0, 0, 0, 0)]
            for n in range(GROUP - 1):
                total += self.group_in[n]
            self.z_in[z] = total
            for dz in (4, 3, 5, 2, 6, 1, 7):
                send(self.z_in.at[z], self.z_in.at[z], *self.sems(1), device(dz=dz))
            leave(self.z_in.at[pl.ds(0, Z - 1)], self.send.at[1])

        def gather(self):
            arrive(self.z_in.at[pl.ds(0, Z - 1)], self.recv.at[1])
            total = self.z_in[0]
            for other in range(1, Z):
                total += self.z_in[other]
            place = self.place(0, 0, 0, 0)
            self.total[place] = total
            for a, b, c, d in group_offsets:
                send(
                    self.total.at[place],
                    self.total.at[place],
                    *self.sems(2),
                    device(dxh=a, dxl=b, dy=c, dco=d),
                )
            leave(self.group_in, self.send.at[2])

        def end(self):
            arrive(self.group_in, self.recv.at[2])

    reduce_third = ShortAllReduce(third, THIRD_ROWS, third_sems)
    reduce_first = AllReduce(first, FIRST_ROWS, first_sems)
    reduce_second = ShortAllReduce(second, SECOND_ROWS, second_sems)

    def first_outputs():
        reduce_first.end()
        loads[5].wait()
        loads[6].wait()
        for k in range(UPPER):
            upper_blocks[k] = upper_diagonal[k] - reduce_first.total[pl.ds(k * BLOCK, BLOCK)]
        for m in range(LOWER):
            wide = parent_panel[m].astype(F32)
            value = -reduce_first.total[pl.ds((UPPER + m) * BLOCK, BLOCK)] - jnp.dot(
                upper_blocks[parents[m]], wide, precision=HIGH, preferred_element_type=F32
            )
            lower_cross[m] = value
            base[m] = lower_diagonal[m] - jnp.dot(
                wide.T, value, precision=HIGH, preferred_element_type=F32
            )
        store(upper_blocks, upper_blocks_hbm)
        store(lower_cross, lower_cross_hbm)

    def outputs(reduction, m0, count):
        reduction.end()
        for m in range(count):
            lower_blocks[m0 + m] = base[m0 + m] - reduction.total[pl.ds(m * BLOCK, BLOCK)]
        ms = pl.ds(m0, count)
        store(lower_blocks.at[ms], lower_blocks_hbm.at[ms])

    def first_multiply(j):
        if SPREAD[j]:
            collect_spread(j)
        if j == min(step[1] for step in ORDER if step[0] == "m0"):
            loads[2].wait()
            loads[3].wait()
        multiply(j, 0)

    first_stages = (reduce_first.core, reduce_first.scatter, reduce_first.exchange,
                    reduce_first.gather, reduce_first.swap, first_outputs)

    def short_stages(reduction, m0, count):
        return (reduction.scatter, reduction.exchange, reduction.gather,
                functools.partial(outputs, reduction, m0, count))

    second_stages = short_stages(reduce_second, 0, LOWER - LATE)
    third_stages = short_stages(reduce_third, LOWER - LATE, LATE)
    work = {
        "seed": seed,
        "ring": ring_event,
        "seed_other": seed_other,
        "m0": first_multiply,
        "m1": lambda j: multiply(j, 1),
        "e": add_core,
        "f": add_y,
        "h": finish,
        "cross": cross,
        "a": lambda i: first_stages[i](),
        "b": lambda i: second_stages[i](),
        "c": lambda i: third_stages[i](),
    }
    for what, *args in ORDER:
        work[what](*args)

    leave(core_out, core_send.at[0])
    leave(y_in, y_send.at[0])
    leave(x_in, x_send.at[0])
    for extent, send_sem in sent:
        pltpu.make_async_remote_copy(
            src_ref=extent, dst_ref=extent, send_sem=send_sem, recv_sem=send_sem,
            device_id=device(dco=1), device_id_type=MESH,
        ).wait_send()
    for copy in stores:
        copy.wait()


def reduce_scratch(rows):
    half = rows // 2
    piece = half // PLANE
    count = 5
    return [
        pltpu.VMEM((half, BLOCK), F32),
        pltpu.VMEM((half, BLOCK), F32),
        pltpu.VMEM((PLANE - 1, piece, BLOCK), F32),
        pltpu.VMEM((Z, piece, BLOCK), F32),
        pltpu.VMEM((rows, BLOCK), F32),
        pltpu.SemaphoreType.DMA((count,)),
        pltpu.SemaphoreType.DMA((count,)),
    ]


def short_reduce_scratch(rows):
    piece = rows // GROUP
    count = 3
    return [
        pltpu.VMEM((GROUP - 1, piece, BLOCK), F32),
        pltpu.VMEM((Z, piece, BLOCK), F32),
        pltpu.VMEM((rows, BLOCK), F32),
        pltpu.SemaphoreType.DMA((count,)),
        pltpu.SemaphoreType.DMA((count,)),
    ]


def finalize(*refs):
    count = len(refs) // 2
    for source, target in zip(refs[:count], refs[count:]):
        target[...] = source[...]


def per_device(
    top_inverse,
    upper_panel,
    upper_pattern,
    upper_diagonal,
    lower_panel,
    lower_pattern,
    parents,
    parent_panel,
    lower_diagonal,
):
    square = (BLOCK, BLOCK)
    anywhere = pl.BlockSpec(memory_space=pl.ANY)
    scalars = pl.BlockSpec(memory_space=pltpu.SMEM)
    vector = pl.BlockSpec(memory_space=pltpu.VMEM)
    out_shape = (
        jax.ShapeDtypeStruct((UPPER, *square), BF16),
        jax.ShapeDtypeStruct((UPPER, *square), F32),
        jax.ShapeDtypeStruct((LOWER, *square), BF16),
        jax.ShapeDtypeStruct((LOWER, *square), F32),
        jax.ShapeDtypeStruct((LOWER, *square), F32),
    )
    outs = pl.pallas_call(
        kernel,
        out_shape=out_shape,
        in_specs=[anywhere, anywhere, scalars, anywhere, anywhere, scalars, scalars, anywhere, anywhere],
        out_specs=(anywhere,) * 5,
        scratch_shapes=[
            *(pltpu.VMEM(array.shape, array.dtype) for array in out_shape),
            pltpu.SemaphoreType.DMA((NC + 4,)),
            pltpu.VMEM((2, COLS, XL * Y, *square), BF16),
            pltpu.VMEM((PANELS, *square), BF16),
            pltpu.VMEM((LOWER, *square), BF16),
            pltpu.VMEM((UPPER, *square), F32),
            pltpu.VMEM((LOWER, *square), F32),
            pltpu.VMEM((PANELS, *square), BF16),
            pltpu.VMEM((COLS, PANELS, *square), BF16),
            pltpu.VMEM((XL * Y, PANELS, *square), BF16),
            pltpu.VMEM((XL * Y, PANELS, *square), BF16),
            pltpu.VMEM((XL * Y, PANELS, *square), F32),
            pltpu.VMEM((XL, Y, PANELS, *square), BF16),
            pltpu.VMEM((Y - 1, XL, PANELS, *square), BF16),
            pltpu.VMEM((XL, PANELS, *square), F32),
            pltpu.VMEM((PANELS, *square), F32),
            pltpu.VMEM((UPPER, *square), BF16),
            pltpu.VMEM((LOWER, *square), F32),
            pltpu.VMEM((LOWER, *square), F32),
            pltpu.VMEM((FIRST_ROWS, BLOCK), F32),
            pltpu.VMEM((SECOND_ROWS, BLOCK), F32),
            pltpu.VMEM((THIRD_ROWS, BLOCK), F32),
            pltpu.SemaphoreType.DMA((7,)),
            pltpu.SemaphoreType.DMA((NC,)),
            pltpu.SemaphoreType.DMA((NC, 2, UP)),
            pltpu.SemaphoreType.DMA((NC,)),
            pltpu.SemaphoreType.DMA((1,)),
            pltpu.SemaphoreType.DMA((NC,)),
            pltpu.SemaphoreType.DMA((1,)),
            pltpu.SemaphoreType.DMA((NC,)),
            pltpu.SemaphoreType.DMA((1,)),
            pltpu.SemaphoreType.DMA((NC,)),
            reduce_scratch(FIRST_ROWS),
            short_reduce_scratch(SECOND_ROWS),
            short_reduce_scratch(THIRD_ROWS),
        ],
        compiler_params=pltpu.CompilerParams(
            collective_id=0, has_side_effects=True, vmem_limit_bytes=62 * 1024 * 1024
        ),
        name="sweep",
    )(
        top_inverse.reshape(COLS, XL * Y, 2, *square),
        upper_panel.reshape(UPPER, *square),
        upper_pattern.reshape(UPPER),
        upper_diagonal,
        lower_panel.reshape(LOWER, *square),
        lower_pattern.reshape(LOWER),
        parents,
        parent_panel,
        lower_diagonal,
    )
    outs = pl.pallas_call(
        finalize,
        out_shape=out_shape,
        in_specs=[vector] * 5,
        out_specs=(vector,) * 5,
        name="finalize",
    )(*outs)
    return (
        outs[0].reshape(UPPER, 1, 1, *square),
        outs[1],
        outs[2].reshape(LOWER, 1, 1, *square),
        outs[3],
        outs[4],
    )


def solution(mesh):
    return jax.shard_map(
        per_device,
        mesh=mesh,
        in_specs=(
            P("row", None, None, "col", None, None),
            P(None, "row", "col", None, None),
            P(None, "row", "col"),
            P(),
            P(None, "row", "col", None, None),
            P(None, "row", "col"),
            P(),
            P(),
            P(),
        ),
        out_specs=(
            P(None, "row", "col", None, None),
            P(),
            P(None, "row", "col", None, None),
            P(),
            P(),
        ),
        check_vma=False,
    )
```

```python
import functools

import jax
import jax.numpy as jnp
from jax import lax
from jax.experimental import pallas as pl
from jax.experimental.pallas import tpu as pltpu
from jax.sharding import PartitionSpec as P

HIGH = lax.Precision.HIGHEST
MESH = pl.DeviceIdType.MESH
F32 = jnp.float32
BF16 = jnp.bfloat16

XL, Y, XH, Z = 2, 4, 2, 8
COLS = XH * Z
PLANE = XH * XL * Y
BLOCK = 128
UPPER, LOWER = 3, 8
PANELS = UPPER + LOWER
UP, DOWN = Z // 2, Z // 2 - 1

CHUNKS = ((0, 2), (2, 1), (3, 2), (5, 2), (7, 2), (9, 1), (10, 1))
SPREAD = (True, True, False, True, False, True, False)
NC = len(CHUNKS)
LATE = 2
ORDER = (
    ("seed", 0), ("seed", 1), ("seed", 2), ("ring", 0, 0, 1), ("ring", 1, 0, 1),
    ("ring", 2, 0, 1), ("seed_other", 2), ("ring", 0, 0, 2), ("ring", 1, 0, 2),
    ("ring", 2, 0, 2), ("ring", 2, 1, 1), ("ring", 0, 0, 3), ("ring", 1, 0, 3),
    ("ring", 2, 0, 3), ("ring", 2, 1, 2), ("ring", 0, 0, 4), ("ring", 1, 0, 4), ("seed", 3),
    ("ring", 2, 0, 4), ("seed", 4), ("ring", 2, 1, 3), ("m0", 0), ("ring", 3, 0, 1), ("m1", 0),
    ("ring", 2, 1, 4), ("ring", 4, 0, 1), ("seed_other", 4), ("m0", 1), ("m1", 1),
    ("ring", 3, 0, 2), ("e", 0), ("m0", 2), ("ring", 4, 0, 2), ("ring", 4, 1, 1), ("e", 1),
    ("m1", 2), ("ring", 3, 0, 3), ("ring", 4, 0, 3), ("e", 2), ("ring", 4, 1, 2),
    ("ring", 3, 0, 4), ("f", 0), ("ring", 4, 0, 4), ("seed", 5), ("seed", 6), ("ring", 4, 1, 3),
    ("f", 1), ("m0", 3), ("ring", 5, 0, 1), ("ring", 6, 0, 1), ("m1", 3), ("ring", 4, 1, 4),
    ("h", 0), ("m0", 4), ("ring", 5, 0, 2), ("ring", 6, 0, 2), ("seed_other", 6), ("h", 1),
    ("cross",), ("f", 2), ("e", 3), ("a", 0), ("m1", 4), ("ring", 5, 0, 3), ("ring", 6, 0, 3),
    ("ring", 6, 1, 1), ("e", 4), ("ring", 5, 0, 4), ("ring", 6, 0, 4), ("a", 1), ("h", 2),
    ("ring", 6, 1, 2), ("ring", 6, 1, 3), ("m0", 5), ("f", 3), ("m1", 5), ("ring", 6, 1, 4),
    ("m0", 6), ("m1", 6), ("e", 5), ("f", 4), ("h", 3), ("e", 6), ("h", 4), ("b", 0), ("a", 2),
    ("f", 5), ("f", 6), ("h", 5), ("h", 6), ("c", 0), ("a", 3), ("b", 1), ("c", 1), ("b", 2),
    ("a", 4), ("c", 2), ("a", 5), ("b", 3), ("c", 3),
)
FIRST_ROWS = 1536
SECOND_ROWS = (LOWER - LATE) * BLOCK
THIRD_ROWS = LATE * BLOCK
GROUP = 2 * PLANE


def kernel(
    top_hbm,
    upper_hbm,
    upper_pattern,
    upper_diagonal_hbm,
    lower_hbm,
    lower_pattern,
    parents,
    parent_panel_hbm,
    lower_diagonal_hbm,
    upper_columns_hbm,
    upper_blocks_hbm,
    lower_columns_hbm,
    lower_cross_hbm,
    lower_blocks_hbm,
    upper_columns,
    upper_blocks,
    lower_columns,
    lower_cross,
    lower_blocks,
    store_sem,
    top,
    panel,
    parent_panel,
    upper_diagonal,
    lower_diagonal,
    masked,
    gathered,
    core_out,
    core_in,
    own_sum,
    y_out,
    y_in,
    x_sum,
    x_in,
    columns_t,
    extension_t,
    base,
    first,
    second,
    third,
    load_sem,
    ring_send,
    ring_recv,
    spread_recv,
    core_send,
    core_recv,
    y_send,
    y_recv,
    x_send,
    x_recv,
    first_sems,
    second_sems,
    third_sems,
):
    row = lax.axis_index("row")
    col = lax.axis_index("col")
    co = row % 2
    y = (row // 2) % Y
    xl = row // (2 * Y)
    z = col % Z
    xh = col // Z

    def device(dxl=0, dy=0, dco=0, dxh=0, dz=0):
        r = (((xl + dxl) % XL) * Y + (y + dy) % Y) * 2 + (co + dco) % 2
        c = ((xh + dxh) % XH) * Z + (z + dz) % Z
        return (r, c)

    plane_offsets = [
        (dxh, dxl, dy)
        for dxh in range(XH)
        for dxl in range(XL)
        for dy in range(Y)
        if (dxh, dxl, dy) != (0, 0, 0)
    ]

    loads = []

    def load(src, dst):
        copy = pltpu.make_async_copy(src, dst, load_sem.at[len(loads)])
        copy.start()
        loads.append(copy)

    load(upper_hbm, panel.at[pl.ds(0, UPPER)])
    load(lower_hbm, panel.at[pl.ds(UPPER, LOWER)])
    load(top_hbm.at[:, :, 1 - co], top.at[1])
    load(top_hbm.at[:, :, co], top.at[0])
    load(parent_panel_hbm, parent_panel)
    load(upper_diagonal_hbm, upper_diagonal)
    load(lower_diagonal_hbm, lower_diagonal)

    stores = []

    def store(src, dst):
        copy = pltpu.make_async_copy(src, dst, store_sem.at[len(stores)])
        copy.start()
        stores.append(copy)

    barrier = pltpu.get_barrier_semaphore()
    partners = [device(dxh=a, dxl=b, dy=c) for a, b, c in plane_offsets]
    partners += [device(dz=d) for d in range(1, Z)] + [device(dco=1)]
    for partner in partners:
        pl.semaphore_signal(barrier, 1, device_id=partner, device_id_type=MESH)

    loads[0].wait()
    loads[1].wait()
    for k in range(PANELS):
        if k < UPPER:
            mask = upper_pattern[k].astype(F32)
        else:
            mask = lower_pattern[k - UPPER].astype(F32)
        wide = panel[k].astype(F32) * mask
        masked[k] = wide.astype(BF16)
        gathered[col, k] = wide.T.astype(BF16)

    pl.semaphore_wait(barrier, len(partners))

    sent = []

    def send(src, dst, send_sem, recv_sem, to):
        pltpu.make_async_remote_copy(
            src_ref=src, dst_ref=dst, send_sem=send_sem, recv_sem=recv_sem,
            device_id=to, device_id_type=MESH,
        ).start()

    def leave(extent, send_sem):
        sent.append((extent, send_sem))

    def arrive(extent, recv_sem):
        pltpu.make_async_remote_copy(
            src_ref=extent, dst_ref=extent, send_sem=recv_sem, recv_sem=recv_sem,
            device_id=device(dco=1), device_id_type=MESH,
        ).wait_recv()

    def block(j, plane, dz):
        k0, nk = CHUNKS[j]
        index = ((xh + plane) % XH) * Z + (z + dz) % Z
        return gathered.at[index, pl.ds(k0, nk)]

    def blocks(j, count):
        k0, nk = CHUNKS[j]
        return gathered.at[pl.ds(0, count), pl.ds(k0, nk)]

    def spread(j, dz):
        mine = block(j, 0, dz)
        send(mine, mine, ring_send.at[j], spread_recv.at[j], device(dxh=1))

    def ring_event(j, plane, step):
        hops = {1: UP, -1: DOWN} if plane == 0 else {1: DOWN, -1: UP}
        if step:
            ways = [way for way in hops if step <= hops[way]]
            arrive(blocks(j, len(ways)), ring_recv.at[j, plane, step - 1])
            if SPREAD[j]:
                for way in ways:
                    spread(j, -way * step)
        for way in hops:
            if step < hops[way]:
                mine = block(j, plane, -way * step)
                send(mine, mine, ring_send.at[j], ring_recv.at[j, plane, step], device(dz=way))

    def seed(j):
        ring_event(j, 0, 0)
        spread(j, 0)
        leave(blocks(j, COLS - 1), ring_send.at[j])

    def seed_other(j):
        arrive(blocks(j, 1), spread_recv.at[j])
        ring_event(j, 1, 0)

    def collect_spread(j):
        arrive(blocks(j, Z), spread_recv.at[j])

    def multiply(j, part):
        k0, nk = CHUNKS[j]
        ks = pl.ds(k0, nk)

        def product(half, pair):
            left = jnp.concatenate(
                [gathered[i, ks].reshape(nk * BLOCK, BLOCK) for i in range(COLS)], axis=1
            )
            right = jnp.concatenate(
                [top[half, :, 2 * pair + d].reshape(COLS * BLOCK, BLOCK) for d in range(2)],
                axis=1,
            )
            return jnp.dot(left, right, preferred_element_type=F32)

        def theirs(pair, carry):
            out = product(1, pair)
            for d in range(2):
                core_out[2 * pair + d, ks] = (
                    out[:, d * BLOCK : (d + 1) * BLOCK].reshape(nk, BLOCK, BLOCK).astype(BF16)
                )
            return carry

        def ours(pair, carry):
            out = product(0, pair)
            for d in range(2):
                own_sum[2 * pair + d, ks] = out[:, d * BLOCK : (d + 1) * BLOCK].reshape(
                    nk, BLOCK, BLOCK
                )
            return carry

        if part == 0:
            lax.fori_loop(0, XL * Y // 2, theirs, 0)
            send(
                core_out.at[:, ks], core_in.at[:, ks], core_send.at[0], core_recv.at[j],
                device(dco=1),
            )
        else:
            lax.fori_loop(0, XL * Y // 2, ours, 0)

    def add_core(j):
        k0, nk = CHUNKS[j]
        ks = pl.ds(k0, nk)
        arrive(core_in.at[:, ks], core_recv.at[j])

        def body(q, carry):
            total = own_sum[q, ks] + core_in[q, ks].astype(F32)
            own_sum[q, ks] = total
            y_out[q // Y, q % Y, ks] = total.astype(BF16)
            return carry

        lax.fori_loop(0, XL * Y, body, 0)
        for dy in (2, 1, 3):
            send(
                y_out.at[:, (y + dy) % Y, ks],
                y_in.at[dy - 1, :, ks],
                y_send.at[0],
                y_recv.at[j],
                device(dy=dy),
            )

    def add_y(j):
        k0, nk = CHUNKS[j]
        ks = pl.ds(k0, nk)
        arrive(y_in.at[:, :, ks], y_recv.at[j])
        for side in range(XL):
            total = own_sum[side * Y + y, ks]
            for dy in range(1, Y):
                total += y_in[dy - 1, side, ks].astype(F32)
            x_sum[side, ks] = total
        send(
            x_sum.at[1 - xl, ks], x_in.at[ks], x_send.at[0], x_recv.at[j], device(dxl=1)
        )

    def finish(j):
        k0, nk = CHUNKS[j]
        ks = pl.ds(k0, nk)
        arrive(x_in.at[ks], x_recv.at[j])
        for k in range(k0, k0 + nk):
            product_t = x_sum[xl, k] + x_in[k]
            if k < UPPER:
                mask = upper_pattern[k].astype(F32)
                wide = -product_t * mask
                columns_t[k] = wide.astype(BF16)
                natural = wide.T.astype(BF16)
                upper_columns[k] = natural
                first[pl.ds(k * BLOCK, BLOCK)] = jnp.dot(
                    gathered[col, k], natural, preferred_element_type=F32
                )
            else:
                m = k - UPPER
                mask = lower_pattern[m].astype(F32)
                natural = (-(product_t + extension_t[m]) * mask).T.astype(BF16)
                lower_columns[m] = natural
                sums, at_row = (second, m) if m < LOWER - LATE else (third, m - LOWER + LATE)
                sums[pl.ds(at_row * BLOCK, BLOCK)] = jnp.dot(
                    gathered[col, k], natural, preferred_element_type=F32
                )
        if k0 < UPPER:
            store(upper_columns.at[ks], upper_columns_hbm.at[ks])
        else:
            ms = pl.ds(k0 - UPPER, nk)
            store(lower_columns.at[ms], lower_columns_hbm.at[ms])

    def cross():
        loads[4].wait()
        first[pl.ds(PANELS * BLOCK, FIRST_ROWS - PANELS * BLOCK)] = jnp.zeros(
            (FIRST_ROWS - PANELS * BLOCK, BLOCK), F32
        )
        for m in range(LOWER):
            selected_t = columns_t[parents[m]]
            first[pl.ds((UPPER + m) * BLOCK, BLOCK)] = jnp.dot(
                selected_t, masked[UPPER + m], preferred_element_type=F32
            )
            panel_t = parent_panel[m].astype(F32).T.astype(BF16)
            extension_t[m] = jnp.dot(panel_t, selected_t, preferred_element_type=F32)

    class AllReduce:
        def __init__(self, array, rows, refs):
            self.array, self.rows = array, rows
            self.half, self.piece = rows // 2, rows // 2 // PLANE
            self.core_in, self.half_sum, self.plane_in, self.z_in, self.total = refs[:5]
            self.send, self.recv = refs[5:]
            self.mine = (xh * XL + xl) * Y + y

        def sems(self, i):
            return self.send.at[i], self.recv.at[i]

        def rows_of(self, half, index, count):
            return pl.ds(pl.multiple_of(half * self.half + index * self.piece, 8), count)

        def core(self):
            send(
                self.array.at[self.rows_of(1 - co, 0, self.half)],
                self.core_in,
                *self.sems(0),
                device(dco=1),
            )
            leave(self.core_in, self.send.at[0])

        def scatter(self):
            arrive(self.core_in, self.recv.at[0])
            self.half_sum[...] = (
                self.array[self.rows_of(co, 0, self.half)] + self.core_in[...]
            )
            for n, (a, b, c) in enumerate(plane_offsets):
                to = (((xh + a) % XH) * XL + (xl + b) % XL) * Y + (y + c) % Y
                send(
                    self.half_sum.at[self.rows_of(0, to, self.piece)],
                    self.plane_in.at[n],
                    *self.sems(1),
                    device(dxh=a, dxl=b, dy=c),
                )
            leave(self.plane_in, self.send.at[1])

        def exchange(self):
            arrive(self.plane_in, self.recv.at[1])
            total = self.half_sum[self.rows_of(0, self.mine, self.piece)]
            for n in range(PLANE - 1):
                total += self.plane_in[n]
            self.z_in[z] = total
            for dz in (4, 3, 5, 2, 6, 1, 7):
                send(self.z_in.at[z], self.z_in.at[z], *self.sems(2), device(dz=dz))
            leave(self.z_in.at[pl.ds(0, Z - 1)], self.send.at[2])

        def gather(self):
            arrive(self.z_in.at[pl.ds(0, Z - 1)], self.recv.at[2])
            total = self.z_in[0]
            for other in range(1, Z):
                total += self.z_in[other]
            place = self.rows_of(co, self.mine, self.piece)
            self.total[place] = total
            for a, b, c in plane_offsets:
                send(
                    self.total.at[place],
                    self.total.at[place],
                    *self.sems(3),
                    device(dxh=a, dxl=b, dy=c),
                )
            leave(self.plane_in, self.send.at[3])

        def swap(self):
            arrive(self.plane_in, self.recv.at[3])
            ours = self.rows_of(co, 0, self.half)
            send(self.total.at[ours], self.total.at[ours], *self.sems(4), device(dco=1))
            leave(self.core_in, self.send.at[4])

        def end(self):
            arrive(self.core_in, self.recv.at[4])

    group_offsets = [(0, 0, 0, 1)] + [
        (*offset, d) for offset in plane_offsets for d in range(2)
    ]

    class ShortAllReduce:
        def __init__(self, array, rows, refs):
            self.array, self.piece = array, rows // GROUP
            self.group_in, self.z_in, self.total, self.send, self.recv = refs

        def sems(self, i):
            return self.send.at[i], self.recv.at[i]

        def place(self, a, b, c, d):
            index = ((((xh + a) % XH) * XL + (xl + b) % XL) * Y + (y + c) % Y) * 2
            index = index + (co + d) % 2
            return pl.ds(pl.multiple_of(index * self.piece, 8), self.piece)

        def scatter(self):
            for n, (a, b, c, d) in enumerate(group_offsets):
                send(
                    self.array.at[self.place(a, b, c, d)],
                    self.group_in.at[n],
                    *self.sems(0),
                    device(dxh=a, dxl=b, dy=c, dco=d),
                )
            leave(self.group_in, self.send.at[0])

        def exchange(self):
            arrive(self.group_in, self.recv.at[0])
            total = self.array[self.place(0, 0, 0, 0)]
            for n in range(GROUP - 1):
                total += self.group_in[n]
            self.z_in[z] = total
            for dz in (4, 3, 5, 2, 6, 1, 7):
                send(self.z_in.at[z], self.z_in.at[z], *self.sems(1), device(dz=dz))
            leave(self.z_in.at[pl.ds(0, Z - 1)], self.send.at[1])

        def gather(self):
            arrive(self.z_in.at[pl.ds(0, Z - 1)], self.recv.at[1])
            total = self.z_in[0]
            for other in range(1, Z):
                total += self.z_in[other]
            place = self.place(0, 0, 0, 0)
            self.total[place] = total
            for a, b, c, d in group_offsets:
                send(
                    self.total.at[place],
                    self.total.at[place],
                    *self.sems(2),
                    device(dxh=a, dxl=b, dy=c, dco=d),
                )
            leave(self.group_in, self.send.at[2])

        def end(self):
            arrive(self.group_in, self.recv.at[2])

    reduce_third = ShortAllReduce(third, THIRD_ROWS, third_sems)
    reduce_first = AllReduce(first, FIRST_ROWS, first_sems)
    reduce_second = ShortAllReduce(second, SECOND_ROWS, second_sems)

    def first_outputs():
        reduce_first.end()
        loads[5].wait()
        loads[6].wait()
        for k in range(UPPER):
            upper_blocks[k] = upper_diagonal[k] - reduce_first.total[pl.ds(k * BLOCK, BLOCK)]
        for m in range(LOWER):
            wide = parent_panel[m].astype(F32)
            value = -reduce_first.total[pl.ds((UPPER + m) * BLOCK, BLOCK)] - jnp.dot(
                upper_blocks[parents[m]], wide, precision=HIGH, preferred_element_type=F32
            )
            lower_cross[m] = value
            base[m] = lower_diagonal[m] - jnp.dot(
                wide.T, value, precision=HIGH, preferred_element_type=F32
            )
        store(upper_blocks, upper_blocks_hbm)
        store(lower_cross, lower_cross_hbm)

    def outputs(reduction, m0, count):
        reduction.end()
        for m in range(count):
            lower_blocks[m0 + m] = base[m0 + m] - reduction.total[pl.ds(m * BLOCK, BLOCK)]
        ms = pl.ds(m0, count)
        store(lower_blocks.at[ms], lower_blocks_hbm.at[ms])

    def first_multiply(j):
        if SPREAD[j]:
            collect_spread(j)
        if j == min(step[1] for step in ORDER if step[0] == "m0"):
            loads[2].wait()
            loads[3].wait()
        multiply(j, 0)

    first_stages = (reduce_first.core, reduce_first.scatter, reduce_first.exchange,
                    reduce_first.gather, reduce_first.swap, first_outputs)

    def short_stages(reduction, m0, count):
        return (reduction.scatter, reduction.exchange, reduction.gather,
                functools.partial(outputs, reduction, m0, count))

    second_stages = short_stages(reduce_second, 0, LOWER - LATE)
    third_stages = short_stages(reduce_third, LOWER - LATE, LATE)
    work = {
        "seed": seed,
        "ring": ring_event,
        "seed_other": seed_other,
        "m0": first_multiply,
        "m1": lambda j: multiply(j, 1),
        "e": add_core,
        "f": add_y,
        "h": finish,
        "cross": cross,
        "a": lambda i: first_stages[i](),
        "b": lambda i: second_stages[i](),
        "c": lambda i: third_stages[i](),
    }
    for what, *args in ORDER:
        work[what](*args)

    leave(core_out, core_send.at[0])
    leave(y_in, y_send.at[0])
    leave(x_in, x_send.at[0])
    for extent, send_sem in sent:
        pltpu.make_async_remote_copy(
            src_ref=extent, dst_ref=extent, send_sem=send_sem, recv_sem=send_sem,
            device_id=device(dco=1), device_id_type=MESH,
        ).wait_send()
    for copy in stores:
        copy.wait()


def reduce_scratch(rows):
    half = rows // 2
    piece = half // PLANE
    count = 5
    return [
        pltpu.VMEM((half, BLOCK), F32),
        pltpu.VMEM((half, BLOCK), F32),
        pltpu.VMEM((PLANE - 1, piece, BLOCK), F32),
        pltpu.VMEM((Z, piece, BLOCK), F32),
        pltpu.VMEM((rows, BLOCK), F32),
        pltpu.SemaphoreType.DMA((count,)),
        pltpu.SemaphoreType.DMA((count,)),
    ]


def short_reduce_scratch(rows):
    piece = rows // GROUP
    count = 3
    return [
        pltpu.VMEM((GROUP - 1, piece, BLOCK), F32),
        pltpu.VMEM((Z, piece, BLOCK), F32),
        pltpu.VMEM((rows, BLOCK), F32),
        pltpu.SemaphoreType.DMA((count,)),
        pltpu.SemaphoreType.DMA((count,)),
    ]


def finalize(*refs):
    count = len(refs) // 2
    for source, target in zip(refs[:count], refs[count:]):
        target[...] = source[...]


def per_device(
    top_inverse,
    upper_panel,
    upper_pattern,
    upper_diagonal,
    lower_panel,
    lower_pattern,
    parents,
    parent_panel,
    lower_diagonal,
):
    square = (BLOCK, BLOCK)
    anywhere = pl.BlockSpec(memory_space=pl.ANY)
    scalars = pl.BlockSpec(memory_space=pltpu.SMEM)
    vector = pl.BlockSpec(memory_space=pltpu.VMEM)
    out_shape = (
        jax.ShapeDtypeStruct((UPPER, *square), BF16),
        jax.ShapeDtypeStruct((UPPER, *square), F32),
        jax.ShapeDtypeStruct((LOWER, *square), BF16),
        jax.ShapeDtypeStruct((LOWER, *square), F32),
        jax.ShapeDtypeStruct((LOWER, *square), F32),
    )
    outs = pl.pallas_call(
        kernel,
        out_shape=out_shape,
        in_specs=[anywhere, anywhere, scalars, anywhere, anywhere, scalars, scalars, anywhere, anywhere],
        out_specs=(anywhere,) * 5,
        scratch_shapes=[
            *(pltpu.VMEM(array.shape, array.dtype) for array in out_shape),
            pltpu.SemaphoreType.DMA((NC + 4,)),
            pltpu.VMEM((2, COLS, XL * Y, *square), BF16),
            pltpu.VMEM((PANELS, *square), BF16),
            pltpu.VMEM((LOWER, *square), BF16),
            pltpu.VMEM((UPPER, *square), F32),
            pltpu.VMEM((LOWER, *square), F32),
            pltpu.VMEM((PANELS, *square), BF16),
            pltpu.VMEM((COLS, PANELS, *square), BF16),
            pltpu.VMEM((XL * Y, PANELS, *square), BF16),
            pltpu.VMEM((XL * Y, PANELS, *square), BF16),
            pltpu.VMEM((XL * Y, PANELS, *square), F32),
            pltpu.VMEM((XL, Y, PANELS, *square), BF16),
            pltpu.VMEM((Y - 1, XL, PANELS, *square), BF16),
            pltpu.VMEM((XL, PANELS, *square), F32),
            pltpu.VMEM((PANELS, *square), F32),
            pltpu.VMEM((UPPER, *square), BF16),
            pltpu.VMEM((LOWER, *square), F32),
            pltpu.VMEM((LOWER, *square), F32),
            pltpu.VMEM((FIRST_ROWS, BLOCK), F32),
            pltpu.VMEM((SECOND_ROWS, BLOCK), F32),
            pltpu.VMEM((THIRD_ROWS, BLOCK), F32),
            pltpu.SemaphoreType.DMA((7,)),
            pltpu.SemaphoreType.DMA((NC,)),
            pltpu.SemaphoreType.DMA((NC, 2, UP)),
            pltpu.SemaphoreType.DMA((NC,)),
            pltpu.SemaphoreType.DMA((1,)),
            pltpu.SemaphoreType.DMA((NC,)),
            pltpu.SemaphoreType.DMA((1,)),
            pltpu.SemaphoreType.DMA((NC,)),
            pltpu.SemaphoreType.DMA((1,)),
            pltpu.SemaphoreType.DMA((NC,)),
            reduce_scratch(FIRST_ROWS),
            short_reduce_scratch(SECOND_ROWS),
            short_reduce_scratch(THIRD_ROWS),
        ],
        compiler_params=pltpu.CompilerParams(
            collective_id=0, has_side_effects=True, vmem_limit_bytes=62 * 1024 * 1024
        ),
        name="sweep",
    )(
        top_inverse.reshape(COLS, XL * Y, 2, *square),
        upper_panel.reshape(UPPER, *square),
        upper_pattern.reshape(UPPER),
        upper_diagonal,
        lower_panel.reshape(LOWER, *square),
        lower_pattern.reshape(LOWER),
        parents,
        parent_panel,
        lower_diagonal,
    )
    outs = pl.pallas_call(
        finalize,
        out_shape=out_shape,
        in_specs=[vector] * 5,
        out_specs=(vector,) * 5,
        name="finalize",
    )(*outs)
    return (
        outs[0].reshape(UPPER, 1, 1, *square),
        outs[1],
        outs[2].reshape(LOWER, 1, 1, *square),
        outs[3],
        outs[4],
    )


def solution(mesh):
    return jax.shard_map(
        per_device,
        mesh=mesh,
        in_specs=(
            P("row", None, None, "col", None, None),
            P(None, "row", "col", None, None),
            P(None, "row", "col"),
            P(),
            P(None, "row", "col", None, None),
            P(None, "row", "col"),
            P(),
            P(),
            P(),
        ),
        out_specs=(
            P(None, "row", "col", None, None),
            P(),
            P(None, "row", "col", None, None),
            P(),
            P(),
        ),
        check_vma=False,
    )
```
